32 devices in a mesh: layer: 16 (over z, x, core), src: 2 (over y).
Axes of the slice: x: 2, y: 2, z: 4, core: 2. Of those that a mesh axis runs over, the one named last changes fastest.
Arguments:
- down_maps: bfloat16 [16, 1664, 1664], P('layer'), may hold values from -1 to 1
- up_maps: bfloat16 [16, 1664, 1664], P('layer'), may hold values from -1 to 1
- local_traces: bfloat16 [128, 1664], P('src'), may hold values from -6 to 6
- src_depth: int32 [128], P('src'), may hold values from 0 to 15
Outputs:
- traces: bfloat16 [16, 128, 1664], P('layer', 'src')
- residual: bfloat16 [16, 128, 1664], P('layer', 'src')
The draws below stay inside these ranges and needn't reach their ends.
All inputs are finite; a program needn't handle non-finite values.
Results may differ from the reference program's by a relative error of at most 0.035.
Values may be sent and summed in bfloat16 or wider, within the bound.
A program may use at most 64 MiB of HBM per device.

```python
import jax
import jax.numpy as jnp
from jax import lax

W = 1664
LAYER_TOTAL = 16
SOURCES = 128


coupling = 0.2


def transfer_maps(key, salt):
    random_child_keys = jax.random.split(jax.random.fold_in(key, salt), 6)
    slow_share = 0.5
    gentle_mask = jax.random.uniform(random_child_keys[0], (W,)) < slow_share
    slow_rate = jnp.exp(jax.random.uniform(random_child_keys[1], (W,), jnp.float32, jnp.log(0.2), jnp.log(1.0)))
    layer_spread = jnp.exp(jax.random.uniform(random_child_keys[2], (LAYER_TOTAL, 1), jnp.float32, jnp.log(0.7), jnp.log(1.4)))
    gentle_amplitude = jnp.sqrt(jnp.maximum(jnp.exp(-2.0 * slow_rate[None, :] * layer_spread / LAYER_TOTAL) - 0.5 * coupling * coupling, 0.01))
    quick_amplitude = jnp.exp(jax.random.uniform(random_child_keys[3], (LAYER_TOTAL, W), jnp.float32, jnp.log(0.3), jnp.log(0.8)))
    spike_layer_list = jax.random.randint(random_child_keys[4], (3,), 0, LAYER_TOTAL)
    spike_selected = jnp.any(jnp.arange(LAYER_TOTAL)[:, None] == spike_layer_list[None, :], axis=1)
    spike_scale = jnp.where(spike_selected[:, None], 0.7, 1.0)
    diagonal_amplitude = jnp.where(gentle_mask[None, :], gentle_amplitude * spike_scale, quick_amplitude)
    identity = jnp.eye(W, dtype=jnp.float32)
    mixing = jax.random.normal(random_child_keys[5], (LAYER_TOTAL, W, W), jnp.float32) * (coupling / jnp.sqrt(jnp.float32(W)))
    mixing = jnp.clip(mixing, -0.9, 0.9)
    return (mixing * (1.0 - identity) + diagonal_amplitude[:, :, None] * identity).astype(jnp.bfloat16)


def draw_down_maps(key, part):
    return transfer_maps(key, 11)


def draw_up_maps(key, part):
    return transfer_maps(key, 23)


def place_ends(drawn, own_key, least, top_value):
    longest = drawn.shape.index(max(drawn.shape))
    spots = []
    for shift in (0, 1):
        where = [jax.random.randint(jax.random.fold_in(own_key, axis), (), 0, length) for axis, length in enumerate(drawn.shape)]
        where[longest] = (where[longest] + shift) % drawn.shape[longest]
        spots.append(tuple(where))
    return drawn.at[spots[0]].set(least).at[spots[1]].set(top_value)


def block_levels(stream_key, extent, pieces, smallest, largest):
    gain, own = 1.0, jax.random.fold_in(stream_key, 6)
    for position, shards_of in pieces:
        steps = jnp.exp(jax.random.uniform(jax.random.fold_in(own, position), (shards_of,), jnp.float32, smallest / len(pieces), largest / len(pieces)))
        gain = gain * jnp.repeat(steps, extent[position] // shards_of).reshape([-1 if axis == position else 1 for axis in range(len(extent))])
    return gain


def gaussian(key, extent, width, limit, cuts=(), kind=jnp.bfloat16):
    result = jax.random.normal(key, extent, jnp.float32) * width
    if len(cuts) > 0:
        result = block_levels(key, extent, cuts, -0.22, 0.18) * result
    return jnp.clip(result, min=-limit, max=limit).astype(kind)


def setup_inputs(seed: int = 0) -> dict:
    splits = jax.random.split(jax.random.key(seed), 5)
    return {
        "down_maps": draw_down_maps(jax.random.fold_in(splits[4], 71), 0),
        "up_maps": draw_up_maps(jax.random.fold_in(splits[4], 71), 0),
        "local_traces": gaussian(splits[2], (SOURCES, W), 1.0, 6.0, ((0, 2),)),
        "src_depth": place_ends(jax.random.randint(splits[3], (SOURCES,), 0, LAYER_TOTAL), jax.random.fold_in(splits[3], 1), 0, LAYER_TOTAL - 1).astype(jnp.int32),
    }


def reference(down_maps, up_maps, local_traces, src_depth):
    layer_ids = jnp.arange(down_maps.shape[0], dtype=jnp.int32)
    placed = src_depth[None, :] == layer_ids[:, None]
    forcing = jnp.where(placed[:, :, None], local_traces.astype(jnp.float32)[None], jnp.float32(0.0))
    empty_edge = jnp.zeros(local_traces.shape, jnp.bfloat16)

    def sweep_step(state_edge, inputs):
        one_map, one_forcing = inputs
        fresh = one_forcing + jnp.dot(state_edge, one_map, preferred_element_type=jnp.float32)
        return fresh.astype(jnp.bfloat16), fresh

    _, downward = lax.scan(sweep_step, empty_edge, (down_maps, forcing))
    _, upward = lax.scan(sweep_step, empty_edge, (up_maps, forcing), reverse=True)
    combined = downward + upward - forcing
    rounded = combined.astype(jnp.bfloat16)
    zero_layer = jnp.zeros((1,) + rounded.shape[1:], jnp.bfloat16)
    above = jnp.concatenate([zero_layer, rounded[:-1]], axis=0)
    below = jnp.concatenate([rounded[1:], zero_layer], axis=0)

    def neighbour_terms(inputs):
        above_one, below_one, down_one, up_one = inputs
        first = jnp.dot(above_one.astype(jnp.float32), down_one.astype(jnp.float32))
        second = jnp.dot(below_one.astype(jnp.float32), up_one.astype(jnp.float32))
        return first, second

    from_above, from_below = lax.map(neighbour_terms, (above, below, down_maps, up_maps))
    remainder = forcing - combined + from_above + from_below
    return rounded, remainder.astype(jnp.bfloat16)
```

```python
import functools

import jax
import jax.numpy as jnp
from jax import lax
from jax.experimental import pallas as pl
from jax.experimental.pallas import tpu as pltpu
from jax.sharding import PartitionSpec as P

MESH = pl.DeviceIdType.MESH
BATCHES = 4


def kernel(
    n, batches, down_ref, up_ref, local_ref, depth_ref, traces_ref, residual_ref,
    maps, inbox, outbox, sidebox, acc, load_sem, wave_send, wave_recv, side_send, side_recv,
):
    me = lax.axis_index("layer")
    rows = inbox.shape[2]
    has_prev = me > 0
    has_next = me < n - 1
    first = jnp.where(me * 2 < n, 0, 1)

    def load(d):
        return pltpu.make_async_copy(
            (down_ref, up_ref)[d].at[0], maps.at[d], load_sem.at[d]
        )

    @pl.when(first == 0)
    def _():
        load(0).start()
        load(1).start()

    @pl.when(first == 1)
    def _():
        load(1).start()
        load(0).start()

    acc[...] = jnp.zeros_like(acc)
    barrier = pltpu.get_barrier_semaphore()

    @pl.when(has_prev)
    def _():
        pl.semaphore_signal(barrier, inc=1, device_id={"layer": me - 1}, device_id_type=MESH)

    @pl.when(has_next)
    def _():
        pl.semaphore_signal(barrier, inc=1, device_id={"layer": me + 1}, device_id_type=MESH)

    pl.semaphore_wait(barrier, has_prev.astype(jnp.int32) + has_next.astype(jnp.int32))

    def batch_rows(b):
        return pl.ds(pl.multiple_of(b * rows, rows), rows)

    def forcing(b):
        where = depth_ref[batch_rows(b), :] == me
        return jnp.where(where, local_ref[batch_rows(b), :].astype(jnp.float32), 0.0)

    def wave_copy(d, b, to):
        return pltpu.make_async_remote_copy(
            src_ref=outbox.at[d, b], dst_ref=inbox.at[d, b],
            send_sem=wave_send.at[d, b], recv_sem=wave_recv.at[d, b],
            device_id={"layer": to}, device_id_type=MESH,
        )

    def side_copy(d, b, to):
        return pltpu.make_async_remote_copy(
            src_ref=outbox.at[d, b], dst_ref=sidebox.at[d, b],
            send_sem=side_send.at[d, b], recv_sem=side_recv.at[d, b],
            device_id={"layer": to}, device_id_type=MESH,
        )

    def neighbours(d):
        step = 1 - 2 * d
        source, target = me - step, me + step
        has_source = jnp.logical_and(source >= 0, source < n)
        has_target = jnp.logical_and(target >= 0, target < n)
        return source, target, has_source, has_target

    def phase(p, carry):
        d = (first + p) % 2
        source, target, has_source, has_target = neighbours(d)
        pltpu.make_async_copy(down_ref.at[0], maps.at[d], load_sem.at[d]).wait()

        def batch(b, carry):
            @pl.when(has_source)
            def _():
                wave_copy(d, b, target).wait_recv()
                moved = jnp.dot(inbox[d, b], maps[d], preferred_element_type=jnp.float32)
                outbox[d, b] = (forcing(b) + moved).astype(jnp.bfloat16)

            @pl.when(jnp.logical_not(has_source))
            def _():
                outbox[d, b] = forcing(b).astype(jnp.bfloat16)

            @pl.when(has_target)
            def _():
                wave_copy(d, b, target).start()

            @pl.when(has_source)
            def _():
                side_copy(d, b, source).start()

            return carry

        return lax.fori_loop(0, batches, batch, carry)

    lax.fori_loop(0, 2, phase, 0)

    for b in range(batches):
        at = batch_rows(b)
        both = outbox[0, b].astype(jnp.float32) + outbox[1, b].astype(jnp.float32)
        traces_ref[0, at, :] = (both - forcing(b)).astype(jnp.bfloat16)

    def side(p, carry):
        e = (first + p) % 2
        source, target, has_source, has_target = neighbours(e)
        sign = 1 - 2 * e

        def batch(b, carry):
            at = batch_rows(b)

            @pl.when(has_target)
            def _():
                side_copy(e, b, source).wait_recv()
                moved = jnp.dot(sidebox[e, b], maps[1 - e], preferred_element_type=jnp.float32)
                total = acc[at, :] + jnp.where((depth_ref[at, :] - me) * sign <= 0, moved, 0.0)
                acc[at, :] = total
                residual_ref[0, at, :] = total.astype(jnp.bfloat16)

            return carry

        return lax.fori_loop(0, batches, batch, carry)

    lax.fori_loop(0, 2, side, 0)

    for d in range(2):
        source, target, has_source, has_target = neighbours(d)
        for b in range(batches):

            @pl.when(has_target)
            def _():
                wave_copy(d, b, target).wait_send()

            @pl.when(has_source)
            def _():
                side_copy(d, b, source).wait_send()


def shards(down_maps, up_maps, local_traces, src_depth, *, batches=BATCHES):
    source_rows, width = local_traces.shape
    n = lax.axis_size("layer")
    rows = source_rows // batches
    out = jax.ShapeDtypeStruct((1, source_rows, width), jnp.bfloat16)
    vmem = pl.BlockSpec(memory_space=pltpu.VMEM)
    anywhere = pl.BlockSpec(memory_space=pl.ANY)
    box = pltpu.VMEM((2, batches, rows, width), jnp.bfloat16)
    return pl.pallas_call(
        functools.partial(kernel, n, batches),
        out_shape=(out, out),
        in_specs=[anywhere, anywhere, vmem, vmem],
        out_specs=(vmem, vmem),
        scratch_shapes=[
            pltpu.VMEM((2, width, width), jnp.bfloat16),
            box,
            box,
            box,
            pltpu.VMEM((source_rows, width), jnp.float32),
            pltpu.SemaphoreType.DMA((2,)),
        ]
        + [pltpu.SemaphoreType.DMA((2, batches))] * 4,
        compiler_params=pltpu.CompilerParams(collective_id=0, has_side_effects=True),
        name="sweeps",
    )(down_maps, up_maps, local_traces, src_depth[:, None])


def solution(mesh):
    return jax.shard_map(
        shards,
        mesh=mesh,
        in_specs=(P("layer", None, None), P("layer", None, None), P("src", None), P("src")),
        out_specs=(P("layer", "src", None), P("layer", "src", None)),
        check_vma=False,
    )
```

```python
import functools

import jax
import jax.numpy as jnp
from jax import lax
from jax.experimental import pallas as pl
from jax.experimental.pallas import tpu as pltpu
from jax.sharding import PartitionSpec as P

MESH = pl.DeviceIdType.MESH
BATCHES = 4
GRANT = 51 * 2**20


def kernel(
    n, batches, down_ref, up_ref, local_ref, depth_ref, traces_ref, residual_ref,
    column, maps, inbox, outbox, sidebox, acc, load_sem, wave_send, wave_recv, side_send, side_recv,
):
    me = lax.axis_index("layer")
    rows = inbox.shape[2]
    has_prev = me > 0
    has_next = me < n - 1
    first = jnp.where(me * 2 < n, 0, 1)

    def load(d):
        return pltpu.make_async_copy(
            (down_ref, up_ref)[d].at[0], maps.at[d], load_sem.at[d]
        )

    for p in range(2):
        for d in range(2):
            needed = has_prev if d == 0 else has_next

            @pl.when(jnp.logical_and((first + p) % 2 == d, needed))
            def _():
                load(d).start()

    acc[...] = jnp.zeros_like(acc)
    barrier = pltpu.get_barrier_semaphore()

    @pl.when(has_prev)
    def _():
        pl.semaphore_signal(barrier, inc=1, device_id={"layer": me - 1}, device_id_type=MESH)

    @pl.when(has_next)
    def _():
        pl.semaphore_signal(barrier, inc=1, device_id={"layer": me + 1}, device_id_type=MESH)

    pl.semaphore_wait(barrier, has_prev.astype(jnp.int32) + has_next.astype(jnp.int32))

    total_rows = depth_ref.shape[1]
    square = (total_rows, total_rows)
    spread = jnp.broadcast_to(depth_ref[...].astype(jnp.float32), square)
    diagonal = lax.broadcasted_iota(jnp.int32, square, 0) == lax.broadcasted_iota(jnp.int32, square, 1)
    column[...] = jnp.sum(jnp.where(diagonal, spread, 0.0), axis=1, keepdims=True)

    def batch_rows(b):
        return pl.ds(pl.multiple_of(b * rows, rows), rows)

    def forcing(b):
        where = column[batch_rows(b), :] == me.astype(jnp.float32)
        return jnp.where(where, local_ref[batch_rows(b), :].astype(jnp.float32), 0.0)

    def wave_copy(d, b, to):
        return pltpu.make_async_remote_copy(
            src_ref=outbox.at[d, b], dst_ref=inbox.at[d, b],
            send_sem=wave_send.at[d, b], recv_sem=wave_recv.at[d, b],
            device_id={"layer": to}, device_id_type=MESH,
        )

    def side_copy(d, b, to):
        return pltpu.make_async_remote_copy(
            src_ref=outbox.at[d, b], dst_ref=sidebox.at[d, b],
            send_sem=side_send.at[d, b], recv_sem=side_recv.at[d, b],
            device_id={"layer": to}, device_id_type=MESH,
        )

    def neighbours(d):
        step = 1 - 2 * d
        source, target = me - step, me + step
        has_source = jnp.logical_and(source >= 0, source < n)
        has_target = jnp.logical_and(target >= 0, target < n)
        return source, target, has_source, has_target

    def phase(p, carry):
        d = (first + p) % 2
        source, target, has_source, has_target = neighbours(d)

        @pl.when(has_source)
        def _():
            pltpu.make_async_copy(down_ref.at[0], maps.at[d], load_sem.at[d]).wait()

        def batch(b, carry):
            @pl.when(has_source)
            def _():
                wave_copy(d, b, target).wait_recv()
                moved = jnp.dot(inbox[d, b], maps[d], preferred_element_type=jnp.float32)
                outbox[d, b] = (forcing(b) + moved).astype(jnp.bfloat16)

            @pl.when(jnp.logical_not(has_source))
            def _():
                outbox[d, b] = forcing(b).astype(jnp.bfloat16)

            @pl.when(has_target)
            def _():
                wave_copy(d, b, target).start()

            return carry

        lax.fori_loop(0, batches, batch, carry)

        @pl.when(has_source)
        def _():
            for b in range(batches):
                side_copy(d, b, source).start()

        return carry

    lax.fori_loop(0, 2, phase, 0)

    for b in range(batches):
        at = batch_rows(b)
        both = outbox[0, b].astype(jnp.float32) + outbox[1, b].astype(jnp.float32)
        traces_ref[0, at, :] = (both - forcing(b)).astype(jnp.bfloat16)

    def side(p, carry):
        e = (first + p) % 2
        source, target, has_source, has_target = neighbours(e)
        sign = 1 - 2 * e

        def batch(b, carry):
            at = batch_rows(b)

            @pl.when(has_target)
            def _():
                side_copy(e, b, source).wait_recv()
                moved = jnp.dot(sidebox[e, b], maps[1 - e], preferred_element_type=jnp.float32)
                total = acc[at, :] + jnp.where((column[at, :] - me.astype(jnp.float32)) * sign.astype(jnp.float32) <= 0.0, moved, 0.0)
                acc[at, :] = total
                residual_ref[0, at, :] = total.astype(jnp.bfloat16)

            return carry

        return lax.fori_loop(0, batches, batch, carry)

    lax.fori_loop(0, 2, side, 0)

    for d in range(2):
        source, target, has_source, has_target = neighbours(d)
        for b in range(batches):

            @pl.when(has_target)
            def _():
                wave_copy(d, b, target).wait_send()

            @pl.when(has_source)
            def _():
                side_copy(d, b, source).wait_send()


def shards(down_maps, up_maps, local_traces, src_depth, *, batches=BATCHES):
    source_rows, width = local_traces.shape
    n = lax.axis_size("layer")
    rows = source_rows // batches
    out = jax.ShapeDtypeStruct((1, source_rows, width), jnp.bfloat16)
    vmem = pl.BlockSpec(memory_space=pltpu.VMEM)
    anywhere = pl.BlockSpec(memory_space=pltpu.HBM)
    box = pltpu.VMEM((2, batches, rows, width), jnp.bfloat16)
    return pl.pallas_call(
        functools.partial(kernel, n, batches),
        out_shape=(out, out),
        in_specs=[anywhere, anywhere, vmem, vmem],
        out_specs=(vmem, vmem),
        scratch_shapes=[
            pltpu.VMEM((source_rows, 1), jnp.float32),
            pltpu.VMEM((2, width, width), jnp.bfloat16),
            box,
            box,
            box,
            pltpu.VMEM((source_rows, width), jnp.float32),
            pltpu.SemaphoreType.DMA((2,)),
        ]
        + [pltpu.SemaphoreType.DMA((2, batches))] * 4,
        compiler_params=pltpu.CompilerParams(collective_id=0, has_side_effects=True, vmem_limit_bytes=GRANT),
        name="sweeps",
    )(down_maps, up_maps, local_traces, src_depth[None, :])


def solution(mesh):
    return jax.shard_map(
        shards,
        mesh=mesh,
        in_specs=(P("layer", None, None), P("layer", None, None), P("src", None), P("src")),
        out_specs=(P("layer", "src", None), P("layer", "src", None)),
        check_vma=False,
    )
```
